256 devices in a mesh: lang: 16 (over y_hi, x, core), mp: 16 (over z, y_lo).
Axes of the slice: x: 4, y: 4 (y_hi: 2, y_lo: 2; y = y_hi * 2 + y_lo), z: 8, core: 2. Of those that a mesh axis runs over, the one named last changes fastest.
Arguments:
- targets: bfloat16 [16, 1024, 2048], P('lang', 'mp'), may hold values from -6 to 6
- memory: bfloat16 [16, 2048, 2048], P('lang', 'mp')
- norm_gain: float32 [2048], replicated, may hold values from 0.25 to 1.75
- query_weight: bfloat16 [2048, 2048], P(None, 'mp'), may hold values from -0.125 to 0.125
- output_weight: bfloat16 [2048, 2048], P('mp'), may hold values from -0.125 to 0.125
- kv_panels: bfloat16 [112, 2, 2048, 2048], P('lang', None, None, 'mp'), may hold values from -0.125 to 0.125
- lang_of_group: int32 [16], replicated, may hold values from 0 to 111
- lang_row: int32 [112], replicated, may hold values from 0 to 111, each once
- src_len: int32 [16], replicated, may hold values from 512 to 2048, as said below
- tgt_len: int32 [16], replicated, may hold values from 256 to 1024, as said below
Outputs:
- attended: bfloat16 [16, 1024, 2048], P('lang', 'mp')
The draws below stay inside these ranges and needn't reach their ends.
Inputs may be any that keep to these rules, and one draw needn't show every extreme that they name: `src_len`: some group has exactly 2048 live source rows in every draw. `tgt_len`: some group has exactly 1024 live target rows in every draw.
All inputs are finite; a program needn't handle non-finite values.
Results may differ from the reference program's by a relative error of at most 0.018.
The reference program's roundings to bfloat16 on the way count: a program that leaves them out, or rounds other values in their place, can miss the bound.
Values may be sent and summed in bfloat16 or wider, within the bound.
A program may use at most 128 MiB of HBM per device.

```python
import jax
import jax.numpy as jnp
from jax import lax

D = 2048
HEADS = 16
GROUPS = 16
TGT = 1024
SRC = 2048
LANGS = 112
N_MP = 16


def draw_memory(key, part):
    key_a = jax.random.fold_in(jax.random.fold_in(key, 11), 0)
    base = jax.random.normal(key_a, (GROUPS, SRC, D), jnp.float32)
    return base.astype(jnp.bfloat16)


def draw_src_len(key, part):
    key_a, key_b = jax.random.split(jax.random.fold_in(key, 23))
    lens = jax.random.randint(key_a, (GROUPS,), SRC // 4, SRC + 1)
    spot = jax.random.randint(key_b, (), 0, GROUPS)
    return lens.at[spot].set(SRC).astype(jnp.int32)


def draw_tgt_len(key, part):
    key_a, key_b = jax.random.split(jax.random.fold_in(key, 37))
    lens = jax.random.randint(key_a, (GROUPS,), TGT // 4, TGT + 1)
    spot = jax.random.randint(key_b, (), 0, GROUPS)
    return lens.at[spot].set(TGT).astype(jnp.int32)


def touch_ends(drawn, stream_key, low, largest):
    dims = drawn.shape
    place = [jax.random.randint(jax.random.fold_in(stream_key, axis), (), 0, dims[axis]) for axis in range(len(dims))]
    drawn = drawn.at[tuple(place)].set(low)
    longest = dims.index(max(dims))
    place[longest] = (place[longest] + 1) % dims[longest]
    return drawn.at[tuple(place)].set(largest)


def block_levels(stream_key, dims, pieces, low, high):
    def one(dim, blocks):
        draws = jax.random.uniform(jax.random.fold_in(jax.random.fold_in(stream_key, 6), dim), (blocks,), jnp.float32, low / len(pieces), high / len(pieces))
        return jnp.repeat(jnp.exp(draws), dims[dim] // blocks).reshape((-1,) + (1,) * (len(dims) - dim - 1))

    loudness = one(*pieces[0])
    for cut in pieces[1:]:
        loudness = loudness * one(*cut)
    return loudness


def bell_draw(key, extent, spread, bound, pieces=(), kind=jnp.bfloat16):
    factor_of = block_levels(key, extent, pieces, -0.22, 0.18) if pieces else 1.0
    result = jax.random.normal(key, extent, jnp.float32) * spread * factor_of
    return jnp.minimum(jnp.maximum(result, -bound), bound).astype(kind)


def setup_inputs(seed: int = 0) -> dict:
    seeds = jax.random.split(jax.random.key(seed), 11)
    targets = bell_draw(seeds[0], (GROUPS, TGT, D), 1.0, 6.0, ((0, 16), (1, 16)))
    memory = draw_memory(jax.random.fold_in(seeds[10], 71), 0)
    norm_gain = jnp.clip(1.0 + 0.15 * jax.random.normal(seeds[2], (D,), jnp.float32), 0.25, 1.75)
    query_weight = bell_draw(seeds[3], (D, D), D ** -0.5, 0.125, ((1, 16),))
    output_weight = bell_draw(seeds[4], (D, D), D ** -0.5, 0.125, ((0, 16),))
    kv_panels = bell_draw(seeds[5], (LANGS, 2, D, D), D ** -0.5, 0.125, ((0, 16), (3, 16)))
    lang_of_group = touch_ends(jax.random.randint(seeds[6], (GROUPS,), 0, LANGS), jax.random.fold_in(seeds[6], 1), 0, LANGS - 1).astype(jnp.int32)
    lang_row = jax.random.permutation(seeds[7], LANGS).astype(jnp.int32)
    src_len = draw_src_len(jax.random.fold_in(seeds[10], 71), 0)
    tgt_len = draw_tgt_len(jax.random.fold_in(seeds[10], 71), 0)
    return dict(targets=targets, memory=memory, norm_gain=norm_gain, query_weight=query_weight, output_weight=output_weight, kv_panels=kv_panels, lang_of_group=lang_of_group, lang_row=lang_row, src_len=src_len, tgt_len=tgt_len)


def reference(targets, memory, norm_gain, query_weight, output_weight, kv_panels, lang_of_group, lang_row, src_len, tgt_len):
    head_size = D // HEADS
    width = D // N_MP
    per_set = HEADS // N_MP
    scale = head_size ** (-0.5)

    def one_group(items):
        rows, source, lang_id, slen, tlen = items
        panel = kv_panels[lang_row[lang_id]]
        xf = rows.astype(jnp.float32)
        mean = lax.optimization_barrier(jnp.mean(xf, axis=1, keepdims=True))
        var = lax.optimization_barrier(jnp.mean((xf - mean) ** 2, axis=1, keepdims=True))
        normed = ((xf - mean) * lax.rsqrt(var + 1e-05) * norm_gain[None, :]).astype(jnp.bfloat16)
        query = (jnp.dot(normed, query_weight, preferred_element_type=jnp.float32) * scale).astype(jnp.bfloat16)
        keyval = jnp.einsum('sd,cdw->csw', source.astype(jnp.float32), panel.astype(jnp.float32)).astype(jnp.bfloat16)
        valid = jnp.arange(SRC, dtype=jnp.int32) < slen

        def one_set(c):
            start = (c * width).astype(jnp.int32)
            qs = lax.dynamic_slice_in_dim(query, start, width, 1).reshape(TGT, per_set, head_size)
            ks = lax.dynamic_slice_in_dim(keyval[0], start, width, 1).reshape(SRC, per_set, head_size)
            vs = lax.dynamic_slice_in_dim(keyval[1], start, width, 1).reshape(SRC, per_set, head_size)
            wo = lax.dynamic_slice_in_dim(output_weight, start, width, 0)
            scores = jnp.einsum('thd,shd->hts', qs.astype(jnp.float32), ks.astype(jnp.float32))
            masked = jnp.where(valid[None, None, :], scores, jnp.float32(-1e+30))
            top = lax.optimization_barrier(jnp.max(masked, axis=2, keepdims=True))
            expo = jnp.where(valid[None, None, :], jnp.exp(masked - top), jnp.float32(0.0))
            total = lax.optimization_barrier(jnp.sum(expo, axis=2))
            weights = expo.astype(jnp.bfloat16)
            ctx = jnp.einsum('hts,shd->thd', weights.astype(jnp.float32), vs.astype(jnp.float32))
            ctx = (ctx / jnp.transpose(total)[:, :, None]).astype(jnp.bfloat16).reshape(TGT, width)
            return jnp.dot(ctx, wo, preferred_element_type=jnp.float32).astype(jnp.bfloat16)
        partials = lax.map(one_set, jnp.arange(N_MP, dtype=jnp.int32))
        summed = lax.optimization_barrier(jnp.sum(partials.astype(jnp.float32), axis=0))
        keep = jnp.arange(TGT, dtype=jnp.int32) < tlen
        return jnp.where(keep[:, None], summed, jnp.float32(0.0)).astype(jnp.bfloat16)
    return lax.map(one_group, (targets, memory, lang_of_group, src_len, tgt_len))
```

```python
import functools

import jax
import jax.numpy as jnp
from jax import lax
from jax.experimental import pallas as pl
from jax.experimental.pallas import tpu as pltpu
from jax.sharding import PartitionSpec as P

D = 2048
HEAD = 128
LANG_DEV = 7
NX = 4
NZ = 8
MESH = pl.DeviceIdType.MESH
BF = jnp.bfloat16
F32 = jnp.float32
DX = (2, 1, 3, 0)


def place():
    l = lax.axis_index("lang")
    m = lax.axis_index("mp")
    c = lax.rem(l, 2)
    x = lax.rem(lax.div(l, 2), NX)
    yh = lax.div(l, 2 * NX)
    z = lax.div(m, 2)
    yl = lax.rem(m, 2)
    return yh, x, c, z, yl


def dev(yh, x, c, z, yl):
    return ((yh * NX + x) * 2 + c, z * 2 + yl)


def gather_kernel(
    lg, lr, tgt, mem, gain, wq, wo, kv,
    pan, memh, th, wq2, wo2,
    kvv0, kvv1, kvv2, kvv3, tgtv, csend, crecv, x1s, x1r, x2s, x2r, ys, yra, yrb, yrf,
    lsem, ksem, c_s, c_r, x1_s, x1_r, xu_s, xu_r, xm_s, xm_r, y_s, y_r, m_s, m_r, t_s, t_r, w_s, w_r,
):
    kvv = (kvv0, kvv1, kvv2, kvv3)
    yh, x, c, z, yl = place()
    xp, xm = lax.rem(x + 1, NX), lax.rem(x + NX - 1, NX)
    zp, zm = lax.rem(z + 1, NZ), lax.rem(z + NZ - 1, NZ)
    core_to = dev(yh, x, 1 - c, z, yl)
    xto = (dev(yh, xp, c, z, yl), dev(yh, xm, c, z, yl))
    zto = (dev(yh, x, c, zp, yl), dev(yh, x, c, zm, yl))
    mate = dev(yh, x, c, z, 1 - yl)
    away = dev(1 - yh, x, c, z, 1 - yl)

    local = []

    def here(src, dst, sem):
        cp = pltpu.make_async_copy(src, dst, sem)
        cp.start()
        return cp

    kvc = [here(kv.at[:, pl.ds(2 * k, 2)], kvv[k], ksem.at[k]) for k in range(4)]
    tcp = here(tgt, tgtv, lsem.at[0])
    local.append(here(mem, memh.at[z], lsem.at[1]))
    local.append(here(wq, wq2.at[0], lsem.at[2]))
    local.append(here(wo, wo2.at[0], lsem.at[3]))

    barrier = pltpu.get_barrier_semaphore()
    for to in (core_to, *xto, *zto, mate, away):
        pl.semaphore_signal(barrier, inc=1, device_id=to, device_id_type=MESH)
    pl.semaphore_wait(barrier, 7)

    sends = []

    def send(src, dst, ss, rs, to):
        cp = pltpu.make_async_remote_copy(
            src_ref=src, dst_ref=dst, send_sem=ss, recv_sem=rs, device_id=to, device_id_type=MESH
        )
        cp.start()
        sends.append(cp)
        return cp

    def zblock(d, s):
        return lax.rem(z + NZ - s, NZ) if d == 0 else lax.rem(z + s, NZ)

    def zsend(src0, buf, rows, ss, rs, s):
        out = []
        for d in range(2):
            b = zblock(d, s - 1)
            if s < 4:
                src = src0 if s == 1 and src0 is not None else buf.at[b]
                out.append(send(src, buf.at[b], ss.at[d, s - 1], rs.at[d, s - 1], zto[d]))
            else:
                part = pl.ds(d * (rows // 2), rows // 2)
                out.append(send(buf.at[b, part], buf.at[b, part], ss.at[d, 3], rs.at[d, 3], zto[d]))
        return out

    mrows, trows = memh.shape[1], th.shape[1]
    mcp = zsend(mem, memh, mrows, m_s, m_r, 1)
    wcp = [
        send(wq, wq2.at[1], w_s.at[0], w_r.at[0], mate),
        send(wo, wo2.at[1], w_s.at[1], w_r.at[1], mate),
    ]

    tcp.wait()
    for i in range(trows // 16):
        rows = pl.ds(16 * i, 16)
        xf = tgtv[rows, :].astype(F32)
        mean = jnp.mean(xf, axis=1, keepdims=True)
        var = jnp.mean((xf - mean) ** 2, axis=1, keepdims=True)
        th[z, rows, :] = ((xf - mean) * lax.rsqrt(var + 1e-05) * gain[...]).astype(BF)

    def route(gyh, gx, gc):
        g = (gyh * NX + gx) * 2 + gc
        row = lr[lg[g]]
        own = lax.div(row, LANG_DEV)
        slot = row - own * LANG_DEV
        oc = lax.rem(own, 2)
        ox = lax.rem(lax.div(own, 2), NX)
        oyh = lax.div(own, 2 * NX)
        return slot, oc, ox, oyh

    gxs = [lax.rem(x + dx, NX) for dx in DX]
    mine = [[route(gyh, gx, c) for gyh in range(2)] for gx in gxs]
    theirs = [[route(gyh, gx, 1 - c) for gyh in range(2)] for gx in gxs]

    def rows_loop(fn):
        def body(i, _):
            fn(pl.ds(pl.multiple_of(i * 128, 128), 128))
            return 0

        lax.fori_loop(0, 4, body, 0)

    def pick(flag, a, b):
        return lax.select_n(flag, b, a)

    def cand(k, j, gyh, h, r):
        slot, oc, _, _ = mine[j][gyh]
        return pick(oc == c, kvv[k][slot, h, r, :], crecv[k, j, gyh, h, r, :])

    def fill_c(k, js):
        for j in js:
            for gyh in range(2):
                slot = theirs[j][gyh][0]

                def fn(r):
                    for h in range(2):
                        csend[k, j, gyh, h, r, :] = kvv[k][slot, h, r, :]

                rows_loop(fn)

    ccp = []
    for k in range(4):
        kvc[k].wait()
        for p, js in enumerate(((0,), (1, 2, 3))):
            fill_c(k, js)
            part = pl.ds(js[0], len(js))
            ccp.append(
                send(csend.at[k, part], crecv.at[k, part], c_s.at[k, p], c_r.at[k, p], core_to)
            )
        if k == 0:
            tcps = zsend(None, th, trows, t_s, t_r, 1)

    x1cp, xucp, xmcp, ycp = [], [], [], {}

    def do_x1(k):
        ccp[2 * k].wait_recv()
        for gyh in range(2):

            def fn(r):
                for h in range(2):
                    x1s[k, h, gyh, r, :] = cand(k, 0, gyh, h, r)

            rows_loop(fn)
        x1cp.append(
            [send(x1s.at[k, h], x1r.at[k, h], x1_s.at[k, h], x1_r.at[k, h], xto[h]) for h in range(2)]
        )

    def do_x2u(k):
        ccp[2 * k + 1].wait_recv()
        for gyh in range(2):

            def fn(r):
                for d in range(2):
                    x2s[k, d, 1 - d, gyh, r, :] = cand(k, 1 + d, gyh, 1 - d, r)

            rows_loop(fn)
        xucp.append(
            [
                send(
                    x2s.at[k, d, 1 - d], x2r.at[k, d, 1 - d], xu_s.at[k, d], xu_r.at[k, d], xto[d]
                )
                for d in range(2)
            ]
        )

    def do_x2m(k):
        for cp in x1cp[k]:
            cp.wait_recv()
        back = (xm, xp)
        for gyh in range(2):

            def fn(r):
                for d in range(2):
                    ox = mine[1 + d][gyh][2]
                    x2s[k, d, d, gyh, r, :] = pick(
                        ox == back[d], x1r[k, d, gyh, r, :], cand(k, 1 + d, gyh, d, r)
                    )

            rows_loop(fn)
        xmcp.append(
            [
                send(x2s.at[k, d, d], x2r.at[k, d, d], xm_s.at[k, d], xm_r.at[k, d], xto[d])
                for d in range(2)
            ]
        )

    def do_y(k):
        for cp in xucp[k] + xmcp[k]:
            cp.wait_recv()
        for gyh in range(2):
            ox = mine[3][gyh][2]
            dist = lax.rem(ox - x + NX, NX)
            second = (dist == 1, dist != 3)
            ab = jnp.where(yh == gyh, 0, 1)

            def fn(r):
                for h in range(2):
                    far = pick(second[h], x2r[k, 1, h, gyh, r, :], x2r[k, 0, h, gyh, r, :])
                    ys[k, ab, h, r, :] = pick(dist == 0, cand(k, 3, gyh, h, r), far)

            rows_loop(fn)
        ycp[k, 0] = send(ys.at[k, 0], yra.at[k], y_s.at[k, 0], y_r.at[k, 0], mate)
        ycp[k, 1] = send(ys.at[k, 1], yrb.at[k], y_s.at[k, 1], y_r.at[k, 1], away)

    def do_yf(k):
        ycp[k, 1].wait_recv()
        ycp[k, 2] = send(yrb.at[k], yrf.at[k], y_s.at[k, 2], y_r.at[k, 2], mate)

    g_row = lr[lg[(yh * NX + x) * 2 + c]]
    near = lax.div(lax.div(g_row, LANG_DEV), 2 * NX) == yh

    def do_final(k):
        ycp[k, 0].wait_recv()
        ycp[k, 2].wait_recv()

        def fn(r):
            for h in range(2):
                pan[0, 2 * k + h, r, :] = pick(near, ys[k, 0, h, r, :], yrf[k, h, r, :])
                pan[1, 2 * k + h, r, :] = pick(near, yra[k, h, r, :], yrb[k, h, r, :])

        rows_loop(fn)

    zc = [(mcp, tcps)]

    def do_z(s):
        for cp in zc[s - 1][0] + zc[s - 1][1]:
            cp.wait_recv()
        if s == 1:
            for cp in local:
                cp.wait()
        if s < 4:
            zc.append(
                (zsend(None, memh, mrows, m_s, m_r, s + 1), zsend(None, th, trows, t_s, t_r, s + 1))
            )

    do_x1(0)
    for k in range(4):
        do_x2u(k)
        if k < 3:
            do_x1(k + 1)
        do_x2m(k)
        if k >= 1:
            do_y(k - 1)
        do_z(k + 1)
        if k >= 1:
            do_yf(k - 1)
    do_y(3)
    do_final(0)
    do_final(1)
    do_final(2)
    do_yf(3)
    do_final(3)
    for cp in wcp:
        cp.wait_recv()
    for cp in sends:
        cp.wait_send()


def gather_all(lang_of_group, lang_row, tgt, mem, gain, wq, wo, kv):
    anyspec = pl.BlockSpec(memory_space=pl.ANY)
    vm = pl.BlockSpec(memory_space=pltpu.VMEM)
    sm = pl.BlockSpec(memory_space=pltpu.SMEM)
    u = (512, HEAD)
    mr, tr = mem.shape[0], tgt.shape[0]
    dma = pltpu.SemaphoreType.DMA
    return pl.pallas_call(
        gather_kernel,
        out_shape=(
            jax.ShapeDtypeStruct((2, 8, *u), BF),
            jax.ShapeDtypeStruct((NZ, mr, D), BF),
            jax.ShapeDtypeStruct((NZ, tr, D), BF),
            jax.ShapeDtypeStruct((2, D, HEAD), BF),
            jax.ShapeDtypeStruct((2, HEAD, D), BF),
        ),
        in_specs=[sm, sm, anyspec, anyspec, vm, anyspec, anyspec, anyspec],
        out_specs=(vm,) * 5,
        scratch_shapes=[
            *[pltpu.VMEM((LANG_DEV, 2, *u), BF) for _ in range(4)],
            pltpu.VMEM((tr, D), BF),
            pltpu.VMEM((4, 4, 2, 2, *u), BF),
            pltpu.VMEM((4, 4, 2, 2, *u), BF),
            pltpu.VMEM((4, 2, 2, *u), BF),
            pltpu.VMEM((4, 2, 2, *u), BF),
            pltpu.VMEM((4, 2, 2, 2, *u), BF),
            pltpu.VMEM((4, 2, 2, 2, *u), BF),
            pltpu.VMEM((4, 2, 2, *u), BF),
            pltpu.VMEM((4, 2, *u), BF),
            pltpu.VMEM((4, 2, *u), BF),
            pltpu.VMEM((4, 2, *u), BF),
            dma((4,)),
            dma((4,)),
            dma((4, 2)), dma((4, 2)),
            dma((4, 2)), dma((4, 2)),
            dma((4, 2)), dma((4, 2)),
            dma((4, 2)), dma((4, 2)),
            dma((4, 3)), dma((4, 3)),
            dma((2, 4)), dma((2, 4)),
            dma((2, 4)), dma((2, 4)),
            dma((2,)), dma((2,)),
        ],
        compiler_params=pltpu.CompilerParams(
            collective_id=0, has_side_effects=True, vmem_limit_bytes=64000 * 1024
        ),
    )(lang_of_group, lang_row, tgt, mem, gain, wq, wo, kv)


def on_device(
    targets,
    memory,
    norm_gain,
    query_weight,
    output_weight,
    kv_panels,
    lang_of_group,
    lang_row,
    src_len,
    tgt_len,
):
    scale = HEAD ** (-0.5)
    group = lax.axis_index("lang")
    m = lax.axis_index("mp")
    yl = lax.rem(m, 2)
    z = lax.div(m, 2)
    own_src = src_len[group]
    own_tgt = tgt_len[group]
    pan, memh, th, wq2, wo2 = gather_all(
        lang_of_group,
        lang_row,
        targets[0],
        memory[0],
        norm_gain[None, :],
        query_weight,
        output_weight,
        kv_panels.reshape(LANG_DEV, 8, 512, HEAD),
    )
    tr, mr = th.shape[1], memh.shape[1]
    nt, ns = NZ * tr, NZ * mr
    th = th.reshape(nt, D)
    memh = memh.reshape(ns, D)
    swap = [(i, i ^ 1) for i in range(16)]
    q = (jnp.einsum("td,hde->hte", th, wq2, preferred_element_type=F32) * scale).astype(BF)
    q_far = lax.ppermute(q, "mp", swap)
    q_all = jnp.concatenate([q, q_far[::-1]], axis=1)
    keyval = jnp.einsum(
        "sd,hcde->hcse", memh, pan.reshape(2, 2, D, HEAD), preferred_element_type=F32
    ).astype(BF)
    i = jnp.arange(ns, dtype=jnp.int32)
    live = (lax.div(i, mr) * (2 * mr) + yl * mr + lax.rem(i, mr)) < own_src
    s = jnp.einsum("hte,hse->hts", q_all, keyval[:, 0], preferred_element_type=F32)
    s = jnp.where(live[None, None, :], s, F32(-1e30))
    top = jnp.max(s, axis=2, keepdims=True)
    e = jnp.where(live[None, None, :], jnp.exp(s - top), F32(0.0))
    tot = jnp.sum(e, axis=2, keepdims=True)
    ctx = jnp.einsum("hts,hse->hte", e.astype(BF), keyval[:, 1], preferred_element_type=F32) / tot
    away_ctx = lax.ppermute(ctx[:, nt:].astype(BF), "mp", swap)[::-1]
    away_st = lax.ppermute(jnp.concatenate([top[:, nt:], tot[:, nt:]], axis=2), "mp", swap)[::-1]
    t1, l1 = top[:, :nt], tot[:, :nt]
    t2, l2 = away_st[:, :, 0:1], away_st[:, :, 1:2]
    big = jnp.maximum(t1, t2)
    w1, w2 = l1 * jnp.exp(t1 - big), l2 * jnp.exp(t2 - big)
    ctx = ((ctx[:, :nt] * w1 + away_ctx.astype(F32) * w2) / (w1 + w2)).astype(BF)
    part = jnp.einsum("hte,hed->td", ctx, wo2, preferred_element_type=F32).astype(BF)
    groups = [[2 * a + b for a in range(NZ)] for b in range(2)]
    summed = lax.psum_scatter(
        part, "mp", scatter_dimension=0, axis_index_groups=groups, tiled=True
    ).astype(F32)
    row_ids = m * tr + jnp.arange(tr, dtype=jnp.int32)
    keep = row_ids < own_tgt
    return jnp.where(keep[:, None], summed, F32(0.0)).astype(BF)[None]


def solution(mesh):
    placed = (
        P("lang", "mp", None),
        P("lang", "mp", None),
        P(),
        P(None, "mp"),
        P("mp", None),
        P("lang", None, None, "mp"),
        P(),
        P(),
        P(),
        P(),
    )
    return jax.shard_map(
        on_device, mesh=mesh, in_specs=placed, out_specs=P("lang", "mp", None), check_vma=False
    )
```

```python
import functools

import jax
import jax.numpy as jnp
from jax import lax
from jax.experimental import pallas as pl
from jax.experimental.pallas import tpu as pltpu
from jax.sharding import PartitionSpec as P

D = 2048
HEAD = 128
LANG_DEV = 7
NX = 4
NZ = 8
MESH = pl.DeviceIdType.MESH
BF = jnp.bfloat16
F32 = jnp.float32
DX = (2, 1, 3, 0)


def place():
    l = lax.axis_index("lang")
    m = lax.axis_index("mp")
    c = lax.rem(l, 2)
    x = lax.rem(lax.div(l, 2), NX)
    yh = lax.div(l, 2 * NX)
    z = lax.div(m, 2)
    yl = lax.rem(m, 2)
    return yh, x, c, z, yl


def dev(yh, x, c, z, yl):
    return ((yh * NX + x) * 2 + c, z * 2 + yl)


def block_kernel(
    lg, lr, sl, tl, tgt, mem, gain, wq, wo, kv,
    out,
    pan, memh, th, wq2, wo2,
    kvv0, kvv1, kvv2, kvv3, tgtv, csend, crecv, x1s, x1r, x2s, x2r, ys, yra, yrb, yrf,
    q_all, kmat, vmat, acc, st, coef, ss, sr, cs, cr, p, prs, prr,
    lsem, ksem, c_s, c_r, x1_s, x1_r, xu_s, xu_r, xm_s, xm_r, y_s, y_r, m_s, m_r, t_s, t_r, w_s, w_r,
    e_s, e_r, r_s, r_r,
):
    kvv = (kvv0, kvv1, kvv2, kvv3)
    yh, x, c, z, yl = place()
    xp, xm = lax.rem(x + 1, NX), lax.rem(x + NX - 1, NX)
    zp, zm = lax.rem(z + 1, NZ), lax.rem(z + NZ - 1, NZ)
    core_to = dev(yh, x, 1 - c, z, yl)
    xto = (dev(yh, xp, c, z, yl), dev(yh, xm, c, z, yl))
    zto = (dev(yh, x, c, zp, yl), dev(yh, x, c, zm, yl))
    mate = dev(yh, x, c, z, 1 - yl)
    away = dev(1 - yh, x, c, z, 1 - yl)

    local = []

    def here(src, dst, sem):
        cp = pltpu.make_async_copy(src, dst, sem)
        cp.start()
        return cp

    kvc = [here(kv.at[:, pl.ds(2 * k, 2)], kvv[k], ksem.at[k]) for k in range(4)]
    tcp = here(tgt, tgtv, lsem.at[0])
    local.append(here(mem, memh.at[z], lsem.at[1]))
    local.append(here(wq, wq2.at[yl], lsem.at[2]))
    local.append(here(wo, wo2.at[yl], lsem.at[3]))

    barrier = pltpu.get_barrier_semaphore()
    for to in (core_to, *xto, *zto, mate, away):
        pl.semaphore_signal(barrier, inc=1, device_id=to, device_id_type=MESH)
    pl.semaphore_wait(barrier, 7)

    sends = []

    def send(src, dst, ss, rs, to):
        cp = pltpu.make_async_remote_copy(
            src_ref=src, dst_ref=dst, send_sem=ss, recv_sem=rs, device_id=to, device_id_type=MESH
        )
        cp.start()
        sends.append(cp)
        return cp

    def zblock(d, s):
        return lax.rem(z + NZ - s, NZ) if d == 0 else lax.rem(z + s, NZ)

    def zsend(src0, buf, rows, ss, rs, s):
        out = []
        for d in range(2):
            b = zblock(d, s - 1)
            if s < 4:
                src = src0 if s == 1 and src0 is not None else buf.at[b]
                out.append(send(src, buf.at[b], ss.at[d, s - 1], rs.at[d, s - 1], zto[d]))
            else:
                part = pl.ds(d * (rows // 2), rows // 2)
                out.append(send(buf.at[b, part], buf.at[b, part], ss.at[d, 3], rs.at[d, 3], zto[d]))
        return out

    mrows, trows = memh.shape[1], th.shape[1]
    mcp = zsend(mem, memh, mrows, m_s, m_r, 1)
    wcp = [
        send(wq, wq2.at[yl], w_s.at[0], w_r.at[0], mate),
        send(wo, wo2.at[yl], w_s.at[1], w_r.at[1], mate),
    ]

    tcp.wait()
    for i in range(trows // 16):
        rows = pl.ds(16 * i, 16)
        xf = tgtv[rows, :].astype(F32)
        mean = jnp.mean(xf, axis=1, keepdims=True)
        var = jnp.mean((xf - mean) ** 2, axis=1, keepdims=True)
        th[z, rows, :] = ((xf - mean) * lax.rsqrt(var + 1e-05) * gain[...]).astype(BF)

    def route(gyh, gx, gc):
        g = (gyh * NX + gx) * 2 + gc
        row = lr[lg[g]]
        own = lax.div(row, LANG_DEV)
        slot = row - own * LANG_DEV
        oc = lax.rem(own, 2)
        ox = lax.rem(lax.div(own, 2), NX)
        oyh = lax.div(own, 2 * NX)
        return slot, oc, ox, oyh

    gxs = [lax.rem(x + dx, NX) for dx in DX]
    mine = [[route(gyh, gx, c) for gyh in range(2)] for gx in gxs]
    theirs = [[route(gyh, gx, 1 - c) for gyh in range(2)] for gx in gxs]

    def rows_loop(fn):
        def body(i, _):
            fn(pl.ds(pl.multiple_of(i * 128, 128), 128))
            return 0

        lax.fori_loop(0, 4, body, 0)

    def pick(flag, a, b):
        return lax.select_n(flag, b, a)

    def cand(k, j, gyh, h, r):
        slot, oc, _, _ = mine[j][gyh]
        return pick(oc == c, kvv[k][slot, h, r, :], crecv[k, j, gyh, h, r, :])

    def fill_c(k, js):
        for j in js:
            for gyh in range(2):
                slot = theirs[j][gyh][0]

                def fn(r):
                    for h in range(2):
                        csend[k, j, gyh, h, r, :] = kvv[k][slot, h, r, :]

                rows_loop(fn)

    ccp = []
    for k in range(4):
        kvc[k].wait()
        for half, js in enumerate(((0,), (1, 2, 3))):
            fill_c(k, js)
            part = pl.ds(js[0], len(js))
            ccp.append(
                send(csend.at[k, part], crecv.at[k, part], c_s.at[k, half], c_r.at[k, half], core_to)
            )
        if k == 0:
            tcps = zsend(None, th, trows, t_s, t_r, 1)

    x1cp, xucp, xmcp, ycp = [], [], [], {}

    def do_x1(k):
        ccp[2 * k].wait_recv()
        for gyh in range(2):

            def fn(r):
                for h in range(2):
                    x1s[k, h, gyh, r, :] = cand(k, 0, gyh, h, r)

            rows_loop(fn)
        x1cp.append(
            [send(x1s.at[k, h], x1r.at[k, h], x1_s.at[k, h], x1_r.at[k, h], xto[h]) for h in range(2)]
        )

    def do_x2u(k):
        ccp[2 * k + 1].wait_recv()
        for gyh in range(2):

            def fn(r):
                for d in range(2):
                    x2s[k, d, 1 - d, gyh, r, :] = cand(k, 1 + d, gyh, 1 - d, r)

            rows_loop(fn)
        xucp.append(
            [
                send(
                    x2s.at[k, d, 1 - d], x2r.at[k, d, 1 - d], xu_s.at[k, d], xu_r.at[k, d], xto[d]
                )
                for d in range(2)
            ]
        )

    def do_x2m(k):
        for cp in x1cp[k]:
            cp.wait_recv()
        back = (xm, xp)
        for gyh in range(2):

            def fn(r):
                for d in range(2):
                    ox = mine[1 + d][gyh][2]
                    x2s[k, d, d, gyh, r, :] = pick(
                        ox == back[d], x1r[k, d, gyh, r, :], cand(k, 1 + d, gyh, d, r)
                    )

            rows_loop(fn)
        xmcp.append(
            [
                send(x2s.at[k, d, d], x2r.at[k, d, d], xm_s.at[k, d], xm_r.at[k, d], xto[d])
                for d in range(2)
            ]
        )

    def do_y(k):
        for cp in xucp[k] + xmcp[k]:
            cp.wait_recv()
        for gyh in range(2):
            ox = mine[3][gyh][2]
            dist = lax.rem(ox - x + NX, NX)
            second = (dist == 1, dist != 3)
            ab = jnp.where(yh == gyh, 0, 1)

            def fn(r):
                for h in range(2):
                    far = pick(second[h], x2r[k, 1, h, gyh, r, :], x2r[k, 0, h, gyh, r, :])
                    ys[k, ab, h, r, :] = pick(dist == 0, cand(k, 3, gyh, h, r), far)

            rows_loop(fn)
        ycp[k, 0] = send(ys.at[k, 0], yra.at[k], y_s.at[k, 0], y_r.at[k, 0], mate)
        ycp[k, 1] = send(ys.at[k, 1], yrb.at[k], y_s.at[k, 1], y_r.at[k, 1], away)

    def do_yf(k):
        ycp[k, 1].wait_recv()
        ycp[k, 2] = send(yrb.at[k], yrf.at[k], y_s.at[k, 2], y_r.at[k, 2], mate)

    g_row = lr[lg[(yh * NX + x) * 2 + c]]
    near = lax.div(lax.div(g_row, LANG_DEV), 2 * NX) == yh

    def do_final(k):
        ycp[k, 0].wait_recv()
        ycp[k, 2].wait_recv()

        def fn(r):
            for h in range(2):
                pan[yl, 2 * k + h, r, :] = pick(near, ys[k, 0, h, r, :], yrf[k, h, r, :])
                pan[1 - yl, 2 * k + h, r, :] = pick(near, yra[k, h, r, :], yrb[k, h, r, :])

        rows_loop(fn)

    zc = [(mcp, tcps)]

    def do_z(s):
        for cp in zc[s - 1][0] + zc[s - 1][1]:
            cp.wait_recv()
        if s == 1:
            for cp in local:
                cp.wait()
        if s < 4:
            zc.append(
                (zsend(None, memh, mrows, m_s, m_r, s + 1), zsend(None, th, trows, t_s, t_r, s + 1))
            )

    nt, ns = NZ * trows, NZ * mrows
    group = (yh * NX + x) * 2 + c

    def tiles(count, fn):
        def body(i, _):
            fn(i)
            return 0

        lax.fori_loop(0, count, body, 0)

    def dot(a, b):
        return jnp.dot(a, b, preferred_element_type=F32)

    def do_query():
        for cp in wcp[:1]:
            cp.wait_recv()
        zb = 256 // trows

        def fn(i):
            a = th[pl.ds(zb * i, zb)].reshape(256, D)
            w = jnp.concatenate([wq2[0], wq2[1]], axis=1)
            q = (dot(a, w) * (HEAD**-0.5)).astype(BF)
            r = pl.ds(pl.multiple_of(256 * i, 256), 256)
            q_all[0, 0, r, :] = q[:, :HEAD]
            q_all[0, 1, r, :] = q[:, HEAD:]

        tiles(nt // 256, fn)
        return send(q_all.at[0], q_all.at[1], e_s.at[0], e_r.at[0], mate)

    def project(u0, nu, first, last, dst):
        zb = 256 // mrows
        d0 = (u0 % 4) * 512

        def fn(i):
            a = memh[pl.ds(zb * i, zb), :, pl.ds(d0, 512 * nu)].reshape(256, 512 * nu)
            w = [pan[h, pl.ds(u0, nu)].reshape(512 * nu, HEAD) for h in range(2)]
            v = dot(a, jnp.concatenate(w, axis=1))
            r = pl.ds(pl.multiple_of(256 * i, 256), 256)
            if not first:
                v = v + acc[r, :]
            if last:
                dst[0, r, :] = v[:, :HEAD].astype(BF)
                dst[1, r, :] = v[:, HEAD:].astype(BF)
            else:
                acc[r, :] = v

        tiles(ns // 256, fn)

    srows = lax.broadcasted_iota(jnp.int32, (1, ns), 1)
    srows = lax.div(srows, mrows) * (2 * mrows) + yl * mrows + lax.rem(srows, mrows)
    live = srows < sl[group]

    def do_scores(h):
        def fn(i):
            part = lax.div(i, 2)
            r = pl.ds(pl.multiple_of(256 * lax.rem(i, 2), 256), 256)
            s = lax.dot_general(
                q_all[part, h, r, :], kmat[h], (((1,), (1,)), ((), ())), preferred_element_type=F32
            )
            s = jnp.where(live, s, F32(-1e30))
            top = jnp.max(s, axis=1, keepdims=True)
            e = jnp.where(live, jnp.exp(s - top), F32(0.0))
            st[part, r, h : h + 1] = top
            st[part, r, 2 + h : 3 + h] = jnp.sum(e, axis=1, keepdims=True)
            e = e.astype(BF)
            for b in range(ns // 128):
                csend[2 * h + part, b // 2, b % 2, 0, r, :] = e[:, 128 * b : 128 * (b + 1)]

        tiles(4, fn)

    def do_stats_send():
        ss[...] = jnp.transpose(st[1])[:8, :]
        return send(ss, sr, e_s.at[1], e_r.at[1], mate)

    def do_stats(cp):
        cp.wait_recv()
        far = jnp.transpose(jnp.concatenate([sr[...], jnp.zeros((120, nt), F32)], axis=0))
        for h in range(2):
            t1, l1 = st[0, :, h : h + 1], st[0, :, 2 + h : 3 + h]
            t2, l2 = far[:, h : h + 1], far[:, 2 + h : 3 + h]
            big = jnp.maximum(t1, t2)
            w1, w2 = jnp.exp(t1 - big), jnp.exp(t2 - big)
            both = w1 * l1 + w2 * l2
            coef[:, h : h + 1] = w1 / both
            coef[:, 2 + h : 3 + h] = w2 * l2 / both

    def context(h, part, r):
        e = [csend[2 * h + part, b // 2, b % 2, 0, r, :] for b in range(ns // 128)]
        return dot(jnp.concatenate(e, axis=1), vmat[h])

    def do_context_far(h):
        def fn(i):
            r = pl.ds(pl.multiple_of(256 * i, 256), 256)
            cs[h, r, :] = (context(h, 1, r) / st[1, r, 2 + h : 3 + h]).astype(BF)

        tiles(2, fn)
        return send(cs.at[h], cr.at[h], e_s.at[2 + h], e_r.at[2 + h], mate)

    def do_context_own(h):
        def fn(i):
            r = pl.ds(pl.multiple_of(256 * i, 256), 256)
            acc[r, h * HEAD : (h + 1) * HEAD] = context(h, 0, r) * coef[r, h : h + 1]

        tiles(2, fn)

    hw = D // 2

    def do_out(i):
        pair = lax.rem(lax.div(z, 2) + 2 + i, 4)
        r = pl.ds(pl.multiple_of(pair * (2 * trows), 2 * trows), 2 * trows)
        c2 = [
            (
                acc[r, h * HEAD : (h + 1) * HEAD]
                + cr[h, r, :].astype(F32) * coef[r, 2 + h : 3 + h]
            ).astype(BF)
            for h in range(2)
        ]
        o = dot(jnp.concatenate(c2, axis=1), wo2[...].reshape(2 * HEAD, D)).astype(BF)
        for j in range(2):
            for hf in range(2):
                p[2 * pair + j, hf] = o[j * trows : (j + 1) * trows, hf * hw : (hf + 1) * hw]

    rcp = {}

    def rs_send(d, t, hf):
        b = lax.rem(z + NZ + (5 - t), NZ) if d == 0 else lax.rem(z + NZ - (5 - t), NZ)
        if (d, t - 1, hf) in rcp:
            rcp[d, t - 1, hf].wait_recv()
            prs[d, t - 1, hf] = (
                p[b, hf].astype(F32) + prr[d, t - 2, hf].astype(F32)
            ).astype(BF)
            src = prs.at[d, t - 1, hf]
        else:
            src = p.at[b, hf]
        rcp[d, t, hf] = send(
            src, prr.at[d, t - 1, hf], r_s.at[d, t - 1, hf], r_r.at[d, t - 1, hf], zto[d]
        )

    do_x1(0)
    for k in range(4):
        do_x2u(k)
        if k < 3:
            do_x1(k + 1)
        do_x2m(k)
        if k >= 1:
            do_y(k - 1)
        do_z(k + 1)
        if k == 3:
            qcp = do_query()
        if k >= 1:
            do_yf(k - 1)
    do_final(0)
    do_final(1)
    project(0, 4, True, True, kmat)
    do_y(3)
    for cp in ccp:
        cp.wait_send()
    do_final(2)
    project(4, 2, True, False, None)
    qcp.wait_recv()
    do_scores(0)
    do_yf(3)
    do_scores(1)
    scp = do_stats_send()
    do_stats(scp)
    do_final(3)
    project(6, 2, False, True, vmat)
    fcp = [do_context_far(h) for h in range(2)]
    for h in range(2):
        do_context_own(h)
    wcp[1].wait_recv()
    for cp in fcp:
        cp.wait_recv()
    do_out(0)
    rs_send(0, 1, 0)
    rs_send(1, 1, 1)
    tiles(3, lambda i: do_out(i + 1))
    rs_send(0, 2, 1)
    rs_send(1, 2, 0)
    for t in range(2, 5):
        for first in range(2):
            for d in range(2):
                hf = d if first == 0 else 1 - d
                if t == 2 and hf != d:
                    continue
                rs_send(d, t, hf)
    for hf in range(2):
        for d in range(2):
            rcp[d, 4, hf].wait_recv()
        v = p[z, hf].astype(F32) + prr[0, 3, hf].astype(F32) + prr[1, 3, hf].astype(F32)
        row = (2 * z + yl) * trows + lax.broadcasted_iota(jnp.int32, (trows, hw), 0)
        out[:, hf * hw : (hf + 1) * hw] = jnp.where(row < tl[group], v, F32(0.0)).astype(BF)
    done = [id(cp) for cp in ccp]
    for cp in sends:
        if id(cp) not in done:
            cp.wait_send()


def run_block(lang_of_group, lang_row, src_len, tgt_len, tgt, mem, gain, wq, wo, kv):
    anyspec = pl.BlockSpec(memory_space=pl.ANY)
    vm = pl.BlockSpec(memory_space=pltpu.VMEM)
    sm = pl.BlockSpec(memory_space=pltpu.SMEM)
    u = (512, HEAD)
    mr, tr = mem.shape[0], tgt.shape[0]
    nt, ns = NZ * tr, NZ * mr
    dma = pltpu.SemaphoreType.DMA
    vmem = pltpu.VMEM
    return pl.pallas_call(
        block_kernel,
        out_shape=jax.ShapeDtypeStruct((tr, D), BF),
        in_specs=[sm] * 4 + [anyspec, anyspec, vm, anyspec, anyspec, anyspec],
        out_specs=vm,
        scratch_shapes=[
            vmem((2, 8, *u), BF),
            vmem((NZ, mr, D), BF),
            vmem((NZ, tr, D), BF),
            vmem((2, D, HEAD), BF),
            vmem((2, HEAD, D), BF),
            *[vmem((LANG_DEV, 2, *u), BF) for _ in range(4)],
            vmem((tr, D), BF),
            vmem((4, 4, 2, 2, *u), BF),
            vmem((4, 4, 2, 2, *u), BF),
            vmem((4, 2, 2, *u), BF),
            vmem((4, 2, 2, *u), BF),
            vmem((4, 2, 2, 2, *u), BF),
            vmem((4, 2, 2, 2, *u), BF),
            vmem((4, 2, 2, *u), BF),
            vmem((4, 2, *u), BF),
            vmem((4, 2, *u), BF),
            vmem((4, 2, *u), BF),
            vmem((2, 2, nt, HEAD), BF),
            vmem((2, ns, HEAD), BF),
            vmem((2, ns, HEAD), BF),
            vmem((ns, 2 * HEAD), F32),
            vmem((2, nt, 128), F32),
            vmem((nt, 128), F32),
            vmem((8, nt), F32),
            vmem((8, nt), F32),
            vmem((2, nt, HEAD), BF),
            vmem((2, nt, HEAD), BF),
            vmem((NZ, 2, tr, D // 2), BF),
            vmem((2, 4, 2, tr, D // 2), BF),
            vmem((2, 4, 2, tr, D // 2), BF),
            dma((4,)),
            dma((4,)),
            dma((4, 2)), dma((4, 2)),
            dma((4, 2)), dma((4, 2)),
            dma((4, 2)), dma((4, 2)),
            dma((4, 2)), dma((4, 2)),
            dma((4, 3)), dma((4, 3)),
            dma((2, 4)), dma((2, 4)),
            dma((2, 4)), dma((2, 4)),
            dma((2,)), dma((2,)),
            dma((4,)), dma((4,)),
            dma((2, 4, 2)), dma((2, 4, 2)),
        ],
        compiler_params=pltpu.CompilerParams(
            collective_id=0, has_side_effects=True, vmem_limit_bytes=67_043_328
        ),
    )(lang_of_group, lang_row, src_len, tgt_len, tgt, mem, gain, wq, wo, kv)


def on_device(
    targets,
    memory,
    norm_gain,
    query_weight,
    output_weight,
    kv_panels,
    lang_of_group,
    lang_row,
    src_len,
    tgt_len,
):
    return run_block(
        lang_of_group,
        lang_row,
        src_len,
        tgt_len,
        targets[0],
        memory[0],
        norm_gain[None, :],
        query_weight,
        output_weight,
        kv_panels.reshape(LANG_DEV, 8, 512, HEAD),
    )[None]


def solution(mesh):
    placed = (
        P("lang", "mp", None),
        P("lang", "mp", None),
        P(),
        P(None, "mp"),
        P("mp", None),
        P("lang", None, None, "mp"),
        P(),
        P(),
        P(),
        P(),
    )
    return jax.shard_map(
        on_device, mesh=mesh, in_specs=placed, out_specs=P("lang", "mp", None), check_vma=False
    )
```

```python
import functools

import jax
import jax.numpy as jnp
from jax import lax
from jax.experimental import pallas as pl
from jax.experimental.pallas import tpu as pltpu
from jax.sharding import PartitionSpec as P

D = 2048
HEAD = 128
LANG_DEV = 7
NX = 4
NZ = 8
MESH = pl.DeviceIdType.MESH
BF = jnp.bfloat16
F32 = jnp.float32
DX = (2, 1, 3, 0)
NK = 8
U = 2 * D // (2 * NK)


def place():
    l = lax.axis_index("lang")
    m = lax.axis_index("mp")
    c = lax.rem(l, 2)
    x = lax.rem(lax.div(l, 2), NX)
    yh = lax.div(l, 2 * NX)
    z = lax.div(m, 2)
    yl = lax.rem(m, 2)
    return yh, x, c, z, yl


def dev(yh, x, c, z, yl):
    return ((yh * NX + x) * 2 + c, z * 2 + yl)


def block_kernel(
    lg, lr, sl, tl, tgt, mem, gain, wq, wo, kv,
    out,
    pan, memh, th, wq2, wo2,
    kvv0, kvv1, kvv2, kvv3, kvv4, kvv5, kvv6, kvv7, tgtv, csend, crecv, x1s, x1r, x2s, x2r, ys, yra, yrb, yrf,
    q_all, kmat, vmat, acc, st, coef, ss, sr, cs, cr, p, prs, prr,
    lsem, ksem, c_s, c_r, x1_s, x1_r, xu_s, xu_r, xm_s, xm_r, y_s, y_r, m_s, m_r, t_s, t_r, w_s, w_r,
    e_s, e_r, r_s, r_r,
):
    kvv = (kvv0, kvv1, kvv2, kvv3, kvv4, kvv5, kvv6, kvv7)
    yh, x, c, z, yl = place()
    xp, xm = lax.rem(x + 1, NX), lax.rem(x + NX - 1, NX)
    zp, zm = lax.rem(z + 1, NZ), lax.rem(z + NZ - 1, NZ)
    core_to = dev(yh, x, 1 - c, z, yl)
    xto = (dev(yh, xp, c, z, yl), dev(yh, xm, c, z, yl))
    zto = (dev(yh, x, c, zp, yl), dev(yh, x, c, zm, yl))
    mate = dev(yh, x, c, z, 1 - yl)
    away = dev(1 - yh, x, c, z, 1 - yl)

    local = []

    def here(src, dst, sem):
        cp = pltpu.make_async_copy(src, dst, sem)
        cp.start()
        return cp

    kvc = [here(kv.at[:, pl.ds(2 * k, 2)], kvv[k], ksem.at[k]) for k in range(NK)]
    tcp = here(tgt, tgtv, lsem.at[0])
    local.append(here(mem, memh.at[z], lsem.at[1]))
    local.append(here(wq, wq2.at[yl], lsem.at[2]))
    local.append(here(wo, wo2.at[yl], lsem.at[3]))

    barrier = pltpu.get_barrier_semaphore()
    for to in (core_to, *xto, *zto, mate, away):
        pl.semaphore_signal(barrier, inc=1, device_id=to, device_id_type=MESH)
    pl.semaphore_wait(barrier, 7)

    sends = []
    mrows, trows = memh.shape[1], th.shape[1]

    def send(src, dst, ss, rs, to):
        cp = pltpu.make_async_remote_copy(
            src_ref=src, dst_ref=dst, send_sem=ss, recv_sem=rs, device_id=to, device_id_type=MESH
        )
        cp.start()
        sends.append(cp)
        return cp

    def zblock(d, s):
        return lax.rem(z + NZ - s, NZ) if d == 0 else lax.rem(z + s, NZ)

    def zsend(src0, buf, rows, ss, rs, s):
        out = []
        for d in range(2):
            b = zblock(d, s - 1)
            if s < 4:
                src = src0 if s == 1 and src0 is not None else buf.at[b]
                out.append(send(src, buf.at[b], ss.at[d, s - 1], rs.at[d, s - 1], zto[d]))
            else:
                part = pl.ds(d * (rows // 2), rows // 2)
                out.append(send(buf.at[b, part], buf.at[b, part], ss.at[d, 3], rs.at[d, 3], zto[d]))
        return out

    mrows, trows = memh.shape[1], th.shape[1]
    def do_norm():
        tcp.wait()
        for i in range(trows // 16):
            rows = pl.ds(16 * i, 16)
            xf = tgtv[rows, :].astype(F32)
            mean = jnp.mean(xf, axis=1, keepdims=True)
            var = jnp.mean((xf - mean) ** 2, axis=1, keepdims=True)
            th[z, rows, :] = ((xf - mean) * lax.rsqrt(var + 1e-05) * gain[...]).astype(BF)

    def route(gyh, gx, gc):
        g = (gyh * NX + gx) * 2 + gc
        row = lr[lg[g]]
        own = lax.div(row, LANG_DEV)
        slot = row - own * LANG_DEV
        oc = lax.rem(own, 2)
        ox = lax.rem(lax.div(own, 2), NX)
        oyh = lax.div(own, 2 * NX)
        return slot, oc, ox, oyh

    gxs = [lax.rem(x + dx, NX) for dx in DX]
    mine = [[route(gyh, gx, c) for gyh in range(2)] for gx in gxs]
    theirs = [[route(gyh, gx, 1 - c) for gyh in range(2)] for gx in gxs]

    def rows_loop(fn):
        def body(i, _):
            fn(pl.ds(pl.multiple_of(i * 128, 128), 128))
            return 0

        lax.fori_loop(0, U // 128, body, 0)

    def pick(flag, a, b):
        return lax.select_n(flag, b, a)

    def cand(k, j, gyh, h, r):
        slot, oc, _, _ = mine[j][gyh]
        return pick(oc == c, kvv[k][slot, h, r, :], crecv[k, j, gyh, h, r, :])

    def fill_c(k, js):
        for j in js:
            for gyh in range(2):
                slot = theirs[j][gyh][0]

                def fn(r):
                    for h in range(2):
                        csend[k, j, gyh, h, r, :] = kvv[k][slot, h, r, :]

                rows_loop(fn)

    ccp = []

    def do_c(k):
        kvc[k].wait()
        for half, js in enumerate(((0,), (1, 2, 3))):
            fill_c(k, js)
            part = pl.ds(js[0], len(js))
            ccp.append(
                send(csend.at[k, part], crecv.at[k, part], c_s.at[k, half], c_r.at[k, half], core_to)
            )

    x1cp, xucp, xmcp, ycp = [], [], [], {}

    def do_x1(k):
        ccp[2 * k].wait_recv()
        for gyh in range(2):

            def fn(r):
                for h in range(2):
                    x1s[k, h, gyh, r, :] = cand(k, 0, gyh, h, r)

            rows_loop(fn)
        x1cp.append(
            [send(x1s.at[k, h], x1r.at[k, h], x1_s.at[k, h], x1_r.at[k, h], xto[h]) for h in range(2)]
        )

    def do_x2u(k):
        ccp[2 * k + 1].wait_recv()
        for gyh in range(2):

            def fn(r):
                for d in range(2):
                    x2s[k, d, 1 - d, gyh, r, :] = cand(k, 1 + d, gyh, 1 - d, r)

            rows_loop(fn)
        xucp.append(
            [
                send(
                    x2s.at[k, d, 1 - d], x2r.at[k, d, 1 - d], xu_s.at[k, d], xu_r.at[k, d], xto[d]
                )
                for d in range(2)
            ]
        )

    def do_x2m(k):
        for cp in x1cp[k]:
            cp.wait_recv()
        back = (xm, xp)
        for gyh in range(2):

            def fn(r):
                for d in range(2):
                    ox = mine[1 + d][gyh][2]
                    x2s[k, d, d, gyh, r, :] = pick(
                        ox == back[d], x1r[k, d, gyh, r, :], cand(k, 1 + d, gyh, d, r)
                    )

            rows_loop(fn)
        xmcp.append(
            [
                send(x2s.at[k, d, d], x2r.at[k, d, d], xm_s.at[k, d], xm_r.at[k, d], xto[d])
                for d in range(2)
            ]
        )

    def do_y(k):
        for cp in xucp[k] + xmcp[k]:
            cp.wait_recv()
        for gyh in range(2):
            ox = mine[3][gyh][2]
            dist = lax.rem(ox - x + NX, NX)
            second = (dist == 1, dist != 3)
            ab = jnp.where(yh == gyh, 0, 1)

            def fn(r):
                for h in range(2):
                    far = pick(second[h], x2r[k, 1, h, gyh, r, :], x2r[k, 0, h, gyh, r, :])
                    ys[k, ab, h, r, :] = pick(dist == 0, cand(k, 3, gyh, h, r), far)

            rows_loop(fn)
        ycp[k, 0] = send(ys.at[k, 0], yra.at[k], y_s.at[k, 0], y_r.at[k, 0], mate)
        ycp[k, 1] = send(ys.at[k, 1], yrb.at[k], y_s.at[k, 1], y_r.at[k, 1], away)

    def do_yf(k):
        ycp[k, 1].wait_recv()
        ycp[k, 2] = send(yrb.at[k], yrf.at[k], y_s.at[k, 2], y_r.at[k, 2], mate)

    g_row = lr[lg[(yh * NX + x) * 2 + c]]
    near = lax.div(lax.div(g_row, LANG_DEV), 2 * NX) == yh

    def do_final(k):
        ycp[k, 0].wait_recv()
        ycp[k, 2].wait_recv()

        def fn(r):
            for h in range(2):
                pan[yl, 2 * k + h, r, :] = pick(near, ys[k, 0, h, r, :], yrf[k, h, r, :])
                pan[1 - yl, 2 * k + h, r, :] = pick(near, yra[k, h, r, :], yrb[k, h, r, :])

        rows_loop(fn)

    tz, mz = [], []

    def do_t(s):
        for cp in tz[s - 1]:
            cp.wait_recv()
        if s < 4:
            tz.append(zsend(None, th, trows, t_s, t_r, s + 1))

    def do_m(s):
        for cp in mz[s - 1]:
            cp.wait_recv()
        if s == 1:
            for cp in local:
                cp.wait()
        if s < 4:
            mz.append(zsend(None, memh, mrows, m_s, m_r, s + 1))

    nt, ns = NZ * trows, NZ * mrows
    group = (yh * NX + x) * 2 + c

    def tiles(count, fn):
        def body(i, _):
            fn(i)
            return 0

        lax.fori_loop(0, count, body, 0)

    def dot(a, b):
        return jnp.dot(a, b, preferred_element_type=F32)

    def do_query():
        for cp in wcp[:1]:
            cp.wait_recv()
        zb = 256 // trows

        def fn(i):
            a = th[pl.ds(zb * i, zb)].reshape(256, D)
            w = jnp.concatenate([wq2[0], wq2[1]], axis=1)
            q = (dot(a, w) * (HEAD**-0.5)).astype(BF)
            r = pl.ds(pl.multiple_of(256 * i, 256), 256)
            q_all[0, 0, r, :] = q[:, :HEAD]
            q_all[0, 1, r, :] = q[:, HEAD:]

        tiles(nt // 256, fn)
        return send(q_all.at[0], q_all.at[1], e_s.at[0], e_r.at[0], mate)

    def project(u0, nu, first, last, dst):
        zb = 256 // mrows
        d0 = (u0 % NK) * U

        def fn(i):
            a = memh[pl.ds(zb * i, zb), :, pl.ds(d0, U * nu)].reshape(256, U * nu)
            w = [pan[h, pl.ds(u0, nu)].reshape(U * nu, HEAD) for h in range(2)]
            v = dot(a, jnp.concatenate(w, axis=1))
            r = pl.ds(pl.multiple_of(256 * i, 256), 256)
            if not first:
                v = v + acc[r, :]
            if last:
                dst[0, r, :] = v[:, :HEAD].astype(BF)
                dst[1, r, :] = v[:, HEAD:].astype(BF)
            else:
                acc[r, :] = v

        tiles(ns // 256, fn)

    srows = lax.broadcasted_iota(jnp.int32, (1, ns), 1)
    srows = lax.div(srows, mrows) * (2 * mrows) + yl * mrows + lax.rem(srows, mrows)
    live = srows < sl[group]

    def do_scores(h):
        def fn(i):
            part = lax.div(i, 2)
            r = pl.ds(pl.multiple_of(256 * lax.rem(i, 2), 256), 256)
            s = lax.dot_general(
                q_all[part, h, r, :], kmat[h], (((1,), (1,)), ((), ())), preferred_element_type=F32
            )
            s = jnp.where(live, s, F32(-1e30))
            top = jnp.max(s, axis=1, keepdims=True)
            e = jnp.where(live, jnp.exp(s - top), F32(0.0))
            st[part, r, h : h + 1] = top
            st[part, r, 2 + h : 3 + h] = jnp.sum(e, axis=1, keepdims=True)
            e = e.astype(BF)
            for b in range(ns // 128):
                csend[4 * h + i, b // 2, b % 2, 0] = e[:, 128 * b : 128 * (b + 1)]

        tiles(4, fn)

    def do_stats_send():
        ss[...] = jnp.transpose(st[1])[:8, :]
        return send(ss, sr, e_s.at[1], e_r.at[1], mate)

    def do_stats(cp):
        cp.wait_recv()
        far = jnp.transpose(jnp.concatenate([sr[...], jnp.zeros((120, nt), F32)], axis=0))
        for h in range(2):
            t1, l1 = st[0, :, h : h + 1], st[0, :, 2 + h : 3 + h]
            t2, l2 = far[:, h : h + 1], far[:, 2 + h : 3 + h]
            big = jnp.maximum(t1, t2)
            w1, w2 = jnp.exp(t1 - big), jnp.exp(t2 - big)
            both = w1 * l1 + w2 * l2
            coef[:, h : h + 1] = w1 / both
            coef[:, 2 + h : 3 + h] = w2 * l2 / both

    def context(h, i):
        e = [csend[4 * h + i, b // 2, b % 2, 0] for b in range(ns // 128)]
        return dot(jnp.concatenate(e, axis=1), vmat[h])

    def do_context_far(h):
        def fn(i):
            r = pl.ds(pl.multiple_of(256 * i, 256), 256)
            cs[h, r, :] = (context(h, 2 + i) / st[1, r, 2 + h : 3 + h]).astype(BF)

        tiles(2, fn)
        return send(cs.at[h], cr.at[h], e_s.at[2 + h], e_r.at[2 + h], mate)

    def do_context_own(h):
        def fn(i):
            r = pl.ds(pl.multiple_of(256 * i, 256), 256)
            acc[r, h * HEAD : (h + 1) * HEAD] = context(h, i) * coef[r, h : h + 1]

        tiles(2, fn)

    hw = D // 2

    def do_out(i):
        pair = lax.rem(lax.div(z, 2) + 2 + i, 4)
        r = pl.ds(pl.multiple_of(pair * (2 * trows), 2 * trows), 2 * trows)
        c2 = [
            (
                acc[r, h * HEAD : (h + 1) * HEAD]
                + cr[h, r, :].astype(F32) * coef[r, 2 + h : 3 + h]
            ).astype(BF)
            for h in range(2)
        ]
        o = dot(jnp.concatenate(c2, axis=1), wo2[...].reshape(2 * HEAD, D)).astype(BF)
        for j in range(2):
            for hf in range(2):
                p[2 * pair + j, hf] = o[j * trows : (j + 1) * trows, hf * hw : (hf + 1) * hw]

    rcp = {}

    def rs_send(d, t, hf):
        b = lax.rem(z + NZ + (5 - t), NZ) if d == 0 else lax.rem(z + NZ - (5 - t), NZ)
        if (d, t - 1, hf) in rcp:
            rcp[d, t - 1, hf].wait_recv()
            prs[d, t - 1, hf] = (
                p[b, hf].astype(F32) + prr[d, t - 2, hf].astype(F32)
            ).astype(BF)
            src = prs.at[d, t - 1, hf]
        else:
            src = p.at[b, hf]
        rcp[d, t, hf] = send(
            src, prr.at[d, t - 1, hf], r_s.at[d, t - 1, hf], r_r.at[d, t - 1, hf], zto[d]
        )

    do_c(0)
    mz.append(zsend(mem, memh, mrows, m_s, m_r, 1))
    do_x1(0)
    do_c(1)
    do_x2u(0)
    do_c(2)
    do_norm()
    do_x1(1)
    tz.append(zsend(None, th, trows, t_s, t_r, 1))
    wcp = [
        send(wq, wq2.at[yl], w_s.at[0], w_r.at[0], mate),
        send(wo, wo2.at[yl], w_s.at[1], w_r.at[1], mate),
    ]
    do_c(3)
    do_x2m(0)
    for k in range(1, NK):
        do_x2u(k)
        if k + 3 < NK:
            do_c(k + 3)
        if k + 1 < NK:
            do_x1(k + 1)
        do_x2m(k)
        do_y(k - 1)
        if k % 2 == 1:
            do_t((k + 1) // 2)
            if k == NK - 1:
                qcp = do_query()
            do_m((k + 1) // 2)
        do_yf(k - 1)
    half = NK // 2
    for k in range(half):
        do_final(k)
    project(0, NK, True, True, kmat)
    for cp in ccp:
        cp.wait_send()
    for k in range(half, NK - 2):
        do_final(k)
    project(NK, 2 * (half - 2), True, False, None)
    do_y(NK - 1)
    qcp.wait_recv()
    do_scores(0)
    do_yf(NK - 1)
    do_scores(1)
    scp = do_stats_send()
    do_final(NK - 2)
    project(2 * NK - 4, 2, False, False, None)
    do_stats(scp)
    do_final(NK - 1)
    project(2 * NK - 2, 2, False, True, vmat)
    fcp = [do_context_far(h) for h in range(2)]
    for h in range(2):
        do_context_own(h)
    wcp[1].wait_recv()
    for cp in fcp:
        cp.wait_recv()
    do_out(0)
    rs_send(0, 1, 0)
    rs_send(1, 1, 1)
    tiles(3, lambda i: do_out(i + 1))
    rs_send(0, 2, 1)
    rs_send(1, 2, 0)
    for t in range(2, 5):
        for first in range(2):
            for d in range(2):
                hf = d if first == 0 else 1 - d
                if t == 2 and hf != d:
                    continue
                rs_send(d, t, hf)
    for hf in range(2):
        for d in range(2):
            rcp[d, 4, hf].wait_recv()
        v = p[z, hf].astype(F32) + prr[0, 3, hf].astype(F32) + prr[1, 3, hf].astype(F32)
        row = (2 * z + yl) * trows + lax.broadcasted_iota(jnp.int32, (trows, hw), 0)
        out[:, hf * hw : (hf + 1) * hw] = jnp.where(row < tl[group], v, F32(0.0)).astype(BF)
    done = [id(cp) for cp in ccp]
    for cp in sends:
        if id(cp) not in done:
            cp.wait_send()


def run_block(lang_of_group, lang_row, src_len, tgt_len, tgt, mem, gain, wq, wo, kv):
    anyspec = pl.BlockSpec(memory_space=pl.ANY)
    vm = pl.BlockSpec(memory_space=pltpu.VMEM)
    sm = pl.BlockSpec(memory_space=pltpu.SMEM)
    u = (U, HEAD)
    mr, tr = mem.shape[0], tgt.shape[0]
    nt, ns = NZ * tr, NZ * mr
    dma = pltpu.SemaphoreType.DMA
    vmem = pltpu.VMEM
    return pl.pallas_call(
        block_kernel,
        out_shape=jax.ShapeDtypeStruct((tr, D), BF),
        in_specs=[sm] * 4 + [anyspec, anyspec, vm, anyspec, anyspec, anyspec],
        out_specs=vm,
        scratch_shapes=[
            vmem((2, 2 * NK, *u), BF),
            vmem((NZ, mr, D), BF),
            vmem((NZ, tr, D), BF),
            vmem((2, D, HEAD), BF),
            vmem((2, HEAD, D), BF),
            *[vmem((LANG_DEV, 2, *u), BF) for _ in range(NK)],
            vmem((tr, D), BF),
            vmem((NK, 4, 2, 2, *u), BF),
            vmem((NK, 4, 2, 2, *u), BF),
            vmem((NK, 2, 2, *u), BF),
            vmem((NK, 2, 2, *u), BF),
            vmem((NK, 2, 2, 2, *u), BF),
            vmem((NK, 2, 2, 2, *u), BF),
            vmem((NK, 2, 2, *u), BF),
            vmem((NK, 2, *u), BF),
            vmem((NK, 2, *u), BF),
            vmem((NK, 2, *u), BF),
            vmem((2, 2, nt, HEAD), BF),
            vmem((2, ns, HEAD), BF),
            vmem((2, ns, HEAD), BF),
            vmem((ns, 2 * HEAD), F32),
            vmem((2, nt, 128), F32),
            vmem((nt, 128), F32),
            vmem((8, nt), F32),
            vmem((8, nt), F32),
            vmem((2, nt, HEAD), BF),
            vmem((2, nt, HEAD), BF),
            vmem((NZ, 2, tr, D // 2), BF),
            vmem((2, 4, 2, tr, D // 2), BF),
            vmem((2, 4, 2, tr, D // 2), BF),
            dma((4,)),
            dma((NK,)),
            dma((NK, 2)), dma((NK, 2)),
            dma((NK, 2)), dma((NK, 2)),
            dma((NK, 2)), dma((NK, 2)),
            dma((NK, 2)), dma((NK, 2)),
            dma((NK, 3)), dma((NK, 3)),
            dma((2, 4)), dma((2, 4)),
            dma((2, 4)), dma((2, 4)),
            dma((2,)), dma((2,)),
            dma((4,)), dma((4,)),
            dma((2, 4, 2)), dma((2, 4, 2)),
        ],
        compiler_params=pltpu.CompilerParams(
            collective_id=0, has_side_effects=True, vmem_limit_bytes=67_043_328
        ),
    )(lang_of_group, lang_row, src_len, tgt_len, tgt, mem, gain, wq, wo, kv)


def on_device(
    targets,
    memory,
    norm_gain,
    query_weight,
    output_weight,
    kv_panels,
    lang_of_group,
    lang_row,
    src_len,
    tgt_len,
):
    return run_block(
        lang_of_group,
        lang_row,
        src_len,
        tgt_len,
        targets[0],
        memory[0],
        norm_gain[None, :],
        query_weight,
        output_weight,
        kv_panels.reshape(LANG_DEV, 2 * NK, U, HEAD),
    )[None]


def solution(mesh):
    placed = (
        P("lang", "mp", None),
        P("lang", "mp", None),
        P(),
        P(None, "mp"),
        P("mp", None),
        P("lang", None, None, "mp"),
        P(),
        P(),
        P(),
        P(),
    )
    return jax.shard_map(
        on_device, mesh=mesh, in_specs=placed, out_specs=P("lang", "mp", None), check_vma=False
    )
```
